32 devices in a mesh: dp: 4 (over x, core), tensor: 2 (over y), layer: 4 (over z).
Axes of the slice: x: 2, y: 2, z: 4, core: 2. Of those that a mesh axis runs over, the one named last changes fastest.
Arguments:
- saved_inputs: bfloat16 [4, 2048, 8192], P(None, 'dp', ('tensor', 'layer')), may hold values from -6 to 6
- output_grad: bfloat16 [2048, 8192], P('dp', ('tensor', 'layer')), may hold values from -4 to 4
- weights: bfloat16 [4, 8192, 2, 4, 1024], P(None, 'tensor', None, 'layer'), may hold values from -0.0625 to 0.0625
- proj_in: bfloat16 [4, 64, 8192], P(None, None, ('tensor', 'layer')), may hold values from -0.0625 to 0.0625
- proj_out: bfloat16 [4, 64, 8192], P(None, None, ('tensor', 'layer')), may hold values from -0.0625 to 0.0625
- query_grads: bfloat16 [4, 1024, 4096], P('layer', ('dp', 'tensor')), may hold values from -0.00390625 to 0.00390625
- owner_map: int32 [4], replicated, may hold values from 0 to 3, each once
Outputs:
- input_grad: bfloat16 [2048, 8192], P('dp', ('tensor', 'layer'))
- scores: float32 [4, 1024], P('layer', ('dp', 'tensor'))
The draws below stay inside these ranges and needn't reach their ends.
Inputs may be any that keep to these rules, and one draw needn't show every extreme that they name: `owner_map`: each owner is named by exactly one layer.
All inputs are finite; a program needn't handle non-finite values.
Results may differ from the reference program's by a relative error of at most 0.035.
Values may be sent and summed in bfloat16 or wider, within the bound.
A program may use at most 256 MiB of HBM per device.

```python
import jax
import jax.numpy as jnp
from jax import lax

D = 8192
RANK = 64
LEN = 512
LAYERS = 4
TOKENS = 2048
NTRAIN = 4
NQ = 1024
N_TENSOR = 2
N_LAYER = 4


def levels(rng, extent, split, low, largest):
    def one(dim, shards_of):
        steps = jax.random.uniform(jax.random.fold_in(jax.random.fold_in(rng, 6), dim), (shards_of,), jnp.float32, low / len(split), largest / len(split))
        return jnp.repeat(jnp.exp(steps), extent[dim] // shards_of).reshape((-1,) + (1,) * (len(extent) - dim - 1))

    loudness = one(*split[0])
    for cut in split[1:]:
        loudness = loudness * one(*cut)
    return loudness


def scatter_about(key, shape, deviation, reach, shards=(), dtype=jnp.bfloat16):
    factor_of = levels(key, shape, shards, -0.22, 0.18) if shards else 1.0
    entries = jax.random.normal(key, shape, jnp.float32) * deviation * factor_of
    return jnp.minimum(jnp.maximum(entries, -reach), reach).astype(dtype)


def setup_inputs(seed: int = 0) -> dict:
    keys = jax.random.split(jax.random.key(seed), 8)
    return {
        "saved_inputs": scatter_about(keys[0], (LAYERS, TOKENS, D), 1.0, 6.0, ((1, 4), (2, 8))),
        "output_grad": scatter_about(keys[1], (TOKENS, D), 0.5, 4.0, ((0, 4), (1, 8))),
        "weights": scatter_about(keys[2], (LAYERS, D, N_TENSOR, N_LAYER, D // (N_TENSOR * N_LAYER)), D ** -0.5, 0.0625, ((1, 2), (3, 4))),
        "proj_in": scatter_about(keys[3], (LAYERS, RANK, D), D ** -0.5, 0.0625, ((2, 8),)),
        "proj_out": scatter_about(keys[4], (LAYERS, RANK, D), D ** -0.5, 0.0625, ((2, 8),)),
        "query_grads": scatter_about(keys[5], (LAYERS, NQ, RANK * RANK), (RANK * RANK * LEN) ** -0.5, 0.00390625, ((0, 4), (1, 8))),
        "owner_map": jax.random.permutation(keys[6], LAYERS).astype(jnp.int32),
    }


def reference(saved_inputs, output_grad, weights, proj_in, proj_out, query_grads, owner_map):
    layers = weights.shape[0]
    width = D // (N_TENSOR * N_LAYER)
    grad_now = output_grad.astype(jnp.float32)
    grad_bf = output_grad
    factors = [None] * layers
    for level in reversed(range(layers)):
        out_factor = jnp.dot(grad_bf, proj_out[level].T, preferred_element_type=jnp.float32)
        in_factor = jnp.dot(saved_inputs[level], proj_in[level].T, preferred_element_type=jnp.float32)
        factors[level] = (out_factor, in_factor)
        grid_grad = grad_bf.reshape(TOKENS, N_TENSOR, N_LAYER, width)
        summed = jnp.zeros((TOKENS, D), jnp.float32)
        for group in range(N_LAYER):
            columns = grid_grad[:, :, group, :].reshape(TOKENS, N_TENSOR * width)
            weight_cols = weights[level][:, :, group, :].reshape(D, N_TENSOR * width)
            term = lax.dot_general(columns, weight_cols, (((1,), (1,)), ((), ())), preferred_element_type=jnp.float32)
            rounded = lax.optimization_barrier(term.astype(jnp.bfloat16))
            summed = summed + rounded.astype(jnp.float32)
        grad_now = grad_now + summed
        grad_bf = grad_now.astype(jnp.bfloat16)
    scores = jnp.zeros((NTRAIN, NQ), jnp.float32)
    for level in range(layers):
        out_factor, in_factor = factors[level]
        left = out_factor.reshape(NTRAIN, LEN, RANK)
        right = in_factor.reshape(NTRAIN, LEN, RANK)
        blocks = jnp.einsum("eta,etb->eab", left, right, precision=lax.Precision.HIGHEST)
        blocks = blocks.reshape(NTRAIN, RANK * RANK).astype(jnp.bfloat16)
        queries = lax.dynamic_index_in_dim(query_grads, owner_map[level].astype(jnp.int32), 0, keepdims=False)
        scores = scores + lax.dot_general(blocks, queries, (((1,), (1,)), ((), ())), preferred_element_type=jnp.float32)
    return grad_bf, scores
```

```python
import functools

import jax
import jax.numpy as jnp
from jax import lax
from jax.experimental import pallas as pl
from jax.experimental.pallas import tpu as pltpu
from jax.sharding import PartitionSpec as P

LEN = 512
CHUNKS = 2
MESH = pl.DeviceIdType.MESH
VMEM_BYTES = 67_000_000


def stack_kernel(
    dims,
    grad_hbm,
    weight_hbm,
    proj_ref,
    out_hbm,
    factor_ref,
    raw,
    flat,
    feats,
    part,
    from_left,
    from_right,
    total,
    raw_sem,
    io_sem,
    feat_send,
    feat_recv,
    part_send,
    left_recv,
    right_recv,
):
    layers, n_layer, n_tensor, rows, width, block = dims
    last = n_layer - 1
    piece_rows = flat.shape[2]
    blocks = piece_rows // block
    per_level = n_layer * blocks
    n_tile = min(512, piece_rows)
    z = lax.axis_index("layer")
    t = lax.axis_index("tensor")

    def nth_piece(i):
        return jnp.where(2 * z < n_layer, last - i, i)

    def raw_copy(n):
        level = layers - 1 - n // per_level
        i = (n // blocks) % n_layer
        start = pl.multiple_of(nth_piece(i) * piece_rows + (n % blocks) * block, block)
        return pltpu.make_async_copy(
            weight_hbm.at[level, pl.ds(start, block)], raw.at[n % 2], raw_sem.at[n % 2]
        )

    def relay(first, count):
        @pl.loop(first, first + count)
        def _(n):
            raw_copy(n).wait()

            @pl.when(n + 1 < layers * per_level)
            def _():
                raw_copy(n + 1).start()

            level = layers - 1 - n // per_level
            q = nth_piece((n // blocks) % n_layer)
            at = pl.ds(pl.multiple_of((n % blocks) * block, block), block)
            for a in range(n_tensor):
                flat[level % 2, q, at, a * width : (a + 1) * width] = raw[n % 2, :, a, :]

    def feat_copy(level, c, shift):
        return pltpu.make_async_remote_copy(
            src_ref=feats.at[level, c, t],
            dst_ref=feats.at[level, c, t],
            send_sem=feat_send.at[level, c, shift - 1],
            recv_sem=feat_recv.at[level, c, shift - 1],
            device_id={"tensor": lax.rem(t + shift, n_tensor)},
            device_id_type=MESH,
        )

    def right_copy(level, c, q):
        return pltpu.make_async_remote_copy(
            src_ref=part.at[c, q],
            dst_ref=from_left.at[level % 2, c, last - q],
            send_sem=part_send.at[c, q],
            recv_sem=left_recv.at[level % 2, c, last - q],
            device_id={"layer": z + 1},
            device_id_type=MESH,
        )

    def left_copy(level, c, q):
        return pltpu.make_async_remote_copy(
            src_ref=part.at[c, q],
            dst_ref=from_right.at[level % 2, c, q],
            send_sem=part_send.at[c, q],
            recv_sem=right_recv.at[level % 2, c, q],
            device_id={"layer": z - 1},
            device_id_type=MESH,
        )

    def wait_part_sends(c):
        for q in range(n_layer):

            if q > 0:

                @pl.when(q > z)
                def _():
                    right_copy(0, c, q).wait_send()

            if q < last:

                @pl.when(q < z)
                def _():
                    left_copy(0, c, q).wait_send()

    def multiply(level, c, i):
        q = nth_piece(i)

        @pl.loop(0, piece_rows // n_tile)
        def _(j):
            at = pl.ds(pl.multiple_of(j * n_tile, n_tile), n_tile)
            acc = None
            for a in range(n_tensor):
                term = lax.dot_general(
                    feats[level, c, a],
                    flat[level % 2, q, at, a * width : (a + 1) * width],
                    (((1,), (1,)), ((), ())),
                    preferred_element_type=jnp.float32,
                )
                acc = term if acc is None else acc + term
            part[c, q, :, at] = acc.astype(jnp.bfloat16)

        @pl.when((z == 0) & (q > 0))
        def _():
            right_copy(level, c, q).start()

        @pl.when((z == last) & (q < last))
        def _():
            left_copy(level, c, q).start()

    def forward(level, c, s):
        right_piece, left_piece = last - s + z, s - last + z

        @pl.when((z > 0) & (right_piece <= last))
        def _():
            right_copy(level, c, right_piece).wait_recv()

            @pl.when(right_piece > z)
            def _():
                part[c, right_piece] = (
                    part[c, right_piece].astype(jnp.float32)
                    + from_left[level % 2, c, last - right_piece].astype(jnp.float32)
                ).astype(jnp.bfloat16)
                right_copy(level, c, right_piece).start()

        @pl.when((z < last) & (left_piece >= 0))
        def _():
            left_copy(level, c, left_piece).wait_recv()

            @pl.when(left_piece < z)
            def _():
                part[c, left_piece] = (
                    part[c, left_piece].astype(jnp.float32)
                    + from_right[level % 2, c, left_piece].astype(jnp.float32)
                ).astype(jnp.bfloat16)
                left_copy(level, c, left_piece).start()

    def out_copy(c):
        return pltpu.make_async_copy(
            feats.at[0, c, t], out_hbm.at[pl.ds(c * rows, rows)], io_sem.at[c]
        )

    def finish(level, c):
        for shift in range(1, n_tensor):
            feat_copy(level, c, shift).wait_send()
        total[c] = total[c] + part[c, z].astype(jnp.float32)

        @pl.when(z > 0)
        def _():
            total[c] = total[c] + from_left[level % 2, c, last - z].astype(jnp.float32)

        @pl.when(z < last)
        def _():
            total[c] = total[c] + from_right[level % 2, c, z].astype(jnp.float32)

        feats[jnp.maximum(level - 1, 0), c, t] = total[c].astype(jnp.bfloat16)

        @pl.when(level > 0)
        def _():
            for shift in range(1, n_tensor):
                feat_copy(level - 1, c, shift).start()

        @pl.when(level == 0)
        def _():
            out_copy(c).start()

    barrier = pltpu.get_barrier_semaphore()
    for shift in range(1, n_tensor):
        pl.semaphore_signal(
            barrier, inc=1, device_id={"tensor": lax.rem(t + shift, n_tensor)}, device_id_type=MESH
        )

    @pl.when(z > 0)
    def _():
        pl.semaphore_signal(barrier, inc=1, device_id={"layer": z - 1}, device_id_type=MESH)

    @pl.when(z < last)
    def _():
        pl.semaphore_signal(barrier, inc=1, device_id={"layer": z + 1}, device_id_type=MESH)

    raw_copy(0).start()
    for c in range(CHUNKS):
        pltpu.make_async_copy(
            grad_hbm.at[pl.ds(c * rows, rows)], feats.at[layers - 1, c, t], io_sem.at[c]
        ).start()
    pl.semaphore_wait(barrier, n_tensor - 1 + jnp.minimum(z, 1) + jnp.minimum(last - z, 1))

    for c in range(CHUNKS):
        pltpu.make_async_copy(
            grad_hbm.at[pl.ds(c * rows, rows)], feats.at[layers - 1, c, t], io_sem.at[c]
        ).wait()
        for shift in range(1, n_tensor):
            feat_copy(layers - 1, c, shift).start()
        total[c] = feats[layers - 1, c, t].astype(jnp.float32)

    phases = layers * CHUNKS

    @pl.loop(0, phases + 1)
    def _(p):
        level = layers - 1 - p // CHUNKS
        c = p % CHUNKS
        old_level = layers - 1 - (p - 1) // CHUNKS
        old_c = (p + CHUNKS - 1) % CHUNKS

        @pl.when(p > 0)
        def _():
            forward(old_level, old_c, 1)

        @pl.when(p < phases)
        def _():
            @pl.when(p >= CHUNKS)
            def _():
                wait_part_sends(c)

            @pl.loop(0, n_layer)
            def _(i):
                @pl.when(p == 0)
                def _():
                    relay(i * blocks, blocks)

                @pl.when(i == 0)
                def _():
                    for shift in range(1, n_tensor):
                        feat_copy(level, c, shift).wait_recv()

                multiply(level, c, i)

        half = per_level // 2
        quarter = half // 2
        base = (layers - level) * per_level + c * half

        @pl.when((p > 0) & (level > 0) & (p < phases))
        def _():
            @pl.when(p == 1)
            def _():
                relay(per_level, half)

            relay(base, quarter)

        for s in range(2, n_layer - 1):

            @pl.when(p > 0)
            def _():
                forward(old_level, old_c, s)

        @pl.when((p > 0) & (level > 0) & (p < phases))
        def _():
            relay(base + quarter, half - quarter)

        @pl.when(p > 0)
        def _():
            forward(old_level, old_c, last)
            finish(old_level, old_c)

        @pl.when(p < phases)
        def _():
            factor_ref[level, pl.ds(pl.multiple_of(c * rows, rows), rows), :] = lax.dot_general(
                feats[level, c, t],
                proj_ref[level],
                (((1,), (1,)), ((), ())),
                preferred_element_type=jnp.float32,
            )

    for c in range(CHUNKS):
        wait_part_sends(c)
        out_copy(c).wait()


def backward_stack(output_grad, weights, proj_out):
    layers, in_rows, n_tensor, width = weights.shape
    tokens = output_grad.shape[0]
    rank = proj_out.shape[1]
    n_layer = lax.axis_size("layer")
    rows = tokens // CHUNKS
    piece_rows = in_rows // n_layer
    block = min(128, piece_rows)
    bf16, f32 = jnp.bfloat16, jnp.float32
    dma = pltpu.SemaphoreType.DMA
    hops = n_layer - 1
    return pl.pallas_call(
        functools.partial(stack_kernel, (layers, n_layer, n_tensor, rows, width, block)),
        out_shape=(
            jax.ShapeDtypeStruct((tokens, width), bf16),
            jax.ShapeDtypeStruct((layers, tokens, rank), f32),
        ),
        in_specs=[
            pl.BlockSpec(memory_space=pl.ANY),
            pl.BlockSpec(memory_space=pl.ANY),
            pl.BlockSpec(memory_space=pltpu.VMEM),
        ],
        out_specs=(pl.BlockSpec(memory_space=pl.ANY), pl.BlockSpec(memory_space=pltpu.VMEM)),
        scratch_shapes=[
            pltpu.VMEM((2, block, n_tensor, width), bf16),
            pltpu.VMEM((2, n_layer, piece_rows, n_tensor * width), bf16),
            pltpu.VMEM((layers, CHUNKS, n_tensor, rows, width), bf16),
            pltpu.VMEM((CHUNKS, n_layer, rows, piece_rows), bf16),
            pltpu.VMEM((2, CHUNKS, hops, rows, piece_rows), bf16),
            pltpu.VMEM((2, CHUNKS, hops, rows, piece_rows), bf16),
            pltpu.VMEM((CHUNKS, rows, width), f32),
            dma((2,)),
            dma((CHUNKS,)),
            dma((layers, CHUNKS, n_tensor - 1)),
            dma((layers, CHUNKS, n_tensor - 1)),
            dma((CHUNKS, n_layer)),
            dma((2, CHUNKS, hops)),
            dma((2, CHUNKS, hops)),
        ],
        compiler_params=pltpu.CompilerParams(
            collective_id=0, has_side_effects=True, vmem_limit_bytes=VMEM_BYTES
        ),
        name="backward_stack",
    )(output_grad, weights, proj_out)


def on_device(saved_inputs, output_grad, weights, proj_in, proj_out, query_grads, owner_map):
    layers = weights.shape[0]
    tok_rows = output_grad.shape[0]
    rank = proj_in.shape[1]
    n_tensor = lax.axis_size("tensor")
    n_layer = lax.axis_size("layer")
    owner = lax.axis_index("layer")
    input_grad, out_factor = backward_stack(output_grad, weights[:, :, :, 0, :], proj_out)
    in_factor = jnp.einsum(
        "ltd,lrd->ltr", saved_inputs, proj_in, preferred_element_type=jnp.float32
    )
    stacked = jnp.concatenate([out_factor, in_factor], axis=2).astype(jnp.bfloat16)
    layer_ids = jnp.arange(layers, dtype=jnp.int32)
    inverse = jnp.sum(
        layer_ids[None, :] * (owner_map[None, :] == layer_ids[:, None]).astype(jnp.int32), axis=1
    )
    sequences = tok_rows // LEN
    block_rows = tok_rows // n_tensor
    by_owner = jnp.take(stacked, inverse, axis=0).reshape(n_layer, n_tensor, block_rows, 2 * rank)
    ordered = jnp.swapaxes(by_owner, 0, 1).reshape(n_tensor * n_layer, block_rows, 2 * rank)
    mine = lax.psum_scatter(
        ordered, ("tensor", "layer"), scatter_dimension=0, tiled=True
    ).astype(jnp.float32)[0]
    first_row = lax.axis_index("tensor") * block_rows
    row_seq = (first_row + jnp.arange(block_rows, dtype=jnp.int32)) // LEN
    member = (row_seq[:, None] == jnp.arange(sequences, dtype=jnp.int32)[None, :]).astype(
        jnp.float32
    )
    partial_blocks = jnp.einsum(
        "rs,ra,rb->sab", member, mine[:, :rank], mine[:, rank:], precision=lax.Precision.HIGHEST
    )
    blocks = lax.psum(partial_blocks.reshape(sequences, rank * rank), "tensor")
    blocks_bf = blocks.astype(jnp.bfloat16)
    queries = query_grads[0]
    partial_scores = jnp.einsum(
        "er,qr->eq",
        lax.all_gather(blocks_bf, "dp", axis=0, tiled=True),
        queries,
        preferred_element_type=jnp.float32,
    )
    total = lax.psum(partial_scores, "layer")
    kept = total.shape[0] // n_layer
    scores = lax.dynamic_slice_in_dim(total, owner * kept, kept, 0)
    return (input_grad, scores)


def solution(mesh):
    in_specs = (
        P(None, "dp", ("tensor", "layer")),
        P("dp", ("tensor", "layer")),
        P(None, "tensor", None, "layer", None),
        P(None, None, ("tensor", "layer")),
        P(None, None, ("tensor", "layer")),
        P("layer", ("dp", "tensor"), None),
        P(),
    )
    out_specs = (P("dp", ("tensor", "layer")), P("layer", ("dp", "tensor")))
    return jax.shard_map(
        on_device, mesh=mesh, in_specs=in_specs, out_specs=out_specs, check_vma=False
    )
```
